32 devices in a mesh: lon: 8 (over y, x, core), mem: 4 (over z).
Axes of the slice: x: 2, y: 2, z: 4, core: 2. Of those that a mesh axis runs over, the one named last changes fastest.
Arguments:
- sample_collection: bfloat16 [256, 3, 1, 16, 1024], P('mem', None, None, None, 'lon'), may hold values from -6 to 6
- layer_depth: float32 [1, 16, 1024], P(None, None, 'lon'), may hold values from 0.05 to 0.2
- obs_where: int32 [4, 8, 512], P('mem', 'lon'), may hold values from 0 to 4895, as said below
- observed_values: float32 [4, 8, 512], P('mem', 'lon'), may hold values from -6 to 6
- obs_precision: float32 [4, 8, 512], P('mem', 'lon'), may hold values from 0.5 to 4
- loc_index: int32 [4, 8, 512], P('mem', 'lon'), may hold values from 0 to 15
- obs_count: int32 [4, 8], P('mem', 'lon'), may hold values from 64 to 512, as said below
Outputs:
- analysis: bfloat16 [256, 3, 1, 16, 1024], P('mem', None, None, None, 'lon')
The draws below stay inside these ranges and needn't reach their ends.
Inputs may be any that keep to these rules, and one draw needn't show every extreme that they name: `obs_where`: flat index into a block's region of 3 x 1 x (12) x (136) cells (component, layer, row, column). Slots o < obs_count of a block hold observations; in each draw some block has all 512.
All inputs are finite; a program needn't handle non-finite values.
Results may differ from the reference program's by a relative error of at most 0.0037.
The reference program's roundings to bfloat16 on the way count: a program that leaves them out, or rounds other values in their place, can miss the bound.
Values may be sent and summed in bfloat16 or wider, within the bound.
A program may use at most 128 MiB of HBM per device.

```python
import math
import jax
import jax.numpy as jnp
from jax import lax

MEMBERS = 256
LEV = 1
STEPS = 2
MARGIN_WIDTH = 4
BAND = 4
CLON = 128
NOBS = 512
NS_ITERS = 5
BANDS = 4
STRIPS = 8
LAT = 16
NLON = 1024
N_LON = 8
N_MEM = 4


def draw_obs_where(key, part):
    row_span = BAND + 2 * MARGIN_WIDTH
    column_span = CLON + 2 * MARGIN_WIDTH
    key_field, key_row, key_column = jax.random.split(key, 3)
    layout = (N_MEM, N_LON, NOBS)
    field_pick = jax.random.randint(key_field, layout, 0, 3 * LEV)
    row_pick = jax.random.randint(key_row, layout, 0, row_span)
    column_pick = jax.random.randint(key_column, layout, 0, column_span)
    return ((field_pick * row_span + row_pick) * column_span + column_pick).astype(jnp.int32)


def draw_obs_count(key, part):
    key_base, key_star = jax.random.split(key, 2)
    base_count = jax.random.randint(key_base, (N_MEM, N_LON), NOBS // 8, NOBS + 1)
    chosen = jax.random.randint(key_star, (), 0, N_MEM * N_LON)
    position = jnp.arange(N_MEM * N_LON, dtype=jnp.int32).reshape(N_MEM, N_LON)
    return jnp.where(position == chosen, NOBS, base_count).astype(jnp.int32)


def plant(array, own_key, least, top_value):
    spot = [jax.random.randint(jax.random.fold_in(own_key, axis), (), 0, length) for axis, length in enumerate(array.shape)]
    widest = array.shape.index(max(array.shape))
    neighbour = spot[:widest] + [(spot[widest] + 1) % array.shape[widest]] + spot[widest + 1:]
    return array.at[tuple(spot)].set(least).at[tuple(neighbour)].set(top_value)


def block_levels(rng, extent, cuts, smallest, largest):
    def one(axis_at, blocks):
        heights = jax.random.uniform(jax.random.fold_in(jax.random.fold_in(rng, 6), axis_at), (blocks,), jnp.float32, smallest / len(cuts), largest / len(cuts))
        return jnp.repeat(jnp.exp(heights), extent[axis_at] // blocks).reshape((-1,) + (1,) * (len(extent) - axis_at - 1))

    gain = one(*cuts[0])
    for cut in cuts[1:]:
        gain = gain * one(*cut)
    return gain


def normal_values(rng, shape, deviation, most, cuts=(), kind=jnp.bfloat16):
    drawn = jax.random.normal(rng, shape, jnp.float32) * deviation
    if len(cuts) > 0:
        drawn = block_levels(rng, shape, cuts, -0.22, 0.18) * drawn
    return jnp.clip(drawn, min=-most, max=most).astype(kind)


def setup_inputs(seed: int = 0) -> dict:
    key_list = jax.random.split(jax.random.key(seed), 8)
    return {
        "sample_collection": normal_values(key_list[0], (MEMBERS, 3, LEV, LAT, NLON), 1.0, 6.0, ((0, 4), (4, 8))),
        "layer_depth": jnp.clip(0.05 + 0.15 * jax.random.uniform(key_list[1], (LEV, LAT, NLON), jnp.float32) ** block_levels(key_list[1], (LEV, LAT, NLON), ((2, 8),), -0.2, 0.2), 0.05, 0.2),
        "obs_where": draw_obs_where(jax.random.fold_in(key_list[7], 71), 0),
        "observed_values": normal_values(key_list[3], (BANDS, STRIPS, NOBS), 1.0, 6.0, ((0, 4), (1, 8)), jnp.float32),
        "obs_precision": jnp.clip(jnp.exp(math.log(4.0) - 2.0794415 * jax.random.uniform(key_list[4], (BANDS, STRIPS, NOBS), jnp.float32) ** block_levels(key_list[4], (BANDS, STRIPS, NOBS), ((0, 4), (1, 8)), -0.2, 0.2)), 0.5, 4.0),
        "loc_index": plant(jax.random.randint(key_list[5], (BANDS, STRIPS, NOBS), 0, 16), jax.random.fold_in(key_list[5], 1), 0, 15).astype(jnp.int32),
        "obs_count": draw_obs_count(jax.random.fold_in(key_list[7], 71), 0),
    }


time_step = 0.8
inflation = 1.1

def coriolis_rate(count_rows):
    latitude = jnp.arange(count_rows, dtype=jnp.float32)
    return 0.4 * (latitude / (count_rows - 1) - 0.5)

def lat_diff(field):
    bordered_array = jnp.pad(field, [(0, 0)] * (field.ndim - 2) + [(1, 1), (0, 0)])
    return 0.5 * (bordered_array[..., 2:, :] - bordered_array[..., :-2, :])

def lon_diff(field):
    return 0.5 * (field[..., 2:] - field[..., :-2])

def advance(fields, depth_cut, spin_frequency):
    height = fields[..., 0, :, :, :]
    east_wind = fields[..., 1, :, :, :]
    north_wind = fields[..., 2, :, :, :]
    flux_east = depth_cut * east_wind
    flux_north = depth_cut * north_wind
    height_new = height[..., 1:-1] - time_step * (lon_diff(flux_east) + lat_diff(flux_north)[..., 1:-1])
    east_new = east_wind[..., 2:-2] - time_step * lon_diff(height_new) + time_step * spin_frequency * north_wind[..., 2:-2]
    north_new = north_wind[..., 2:-2] - time_step * lat_diff(height_new)[..., 1:-1] - time_step * spin_frequency * east_wind[..., 2:-2]
    return jnp.stack([height_new[..., 1:-1], east_new, north_new], axis=-4)

def sample_prediction(sample_number, bordered_thickness_grid, spin_frequency):
    reach = 2 * STEPS
    enlarged_grid = jnp.pad(sample_number.astype(jnp.float32), ((0, 0), (0, 0), (0, 0), (reach, reach)), mode='wrap')
    total = bordered_thickness_grid.shape[-1]
    for step_index in range(STEPS):
        enlarged_grid = advance(enlarged_grid, bordered_thickness_grid[..., 2 * step_index:total - 2 * step_index], spin_frequency)
    return enlarged_grid.astype(jnp.bfloat16)

def analyse(region, where, values, precision_vals, locs, count):
    members = region.shape[0]
    highest = lax.Precision.HIGHEST
    flattened = region.reshape(members, -1)
    picked = jnp.take(flattened, where, axis=1).astype(jnp.float32)
    slot_index = jnp.arange(where.shape[0], dtype=jnp.int32)
    live_slots = (slot_index < count).astype(jnp.float32)
    taper_table = (1.0 - jnp.arange(16, dtype=jnp.float32) / 16.0) ** 2
    taper_weight = lax.optimization_barrier(jnp.sum(jnp.where(locs[:, None] == jnp.arange(16, dtype=jnp.int32)[None, :], taper_table[None, :], 0.0), axis=1))
    weight = precision_vals * taper_weight * live_slots
    obs_mean = lax.optimization_barrier(jnp.mean(picked, axis=0))
    spread = picked - obs_mean[None, :]
    innovation = values - obs_mean
    weighted = spread * weight[None, :]
    gram_matrix = jnp.dot(weighted, spread.T, precision=highest)
    drive_vector = jnp.dot(weighted, innovation, precision=highest)
    prior = (members - 1) / inflation
    trace_bound = prior + jnp.trace(gram_matrix)
    identity = jnp.eye(members, dtype=jnp.float32)
    root_iter = (gram_matrix + prior * identity) / trace_bound
    inv_root = identity
    for sweep in range(NS_ITERS):
        correction = 1.5 * identity - 0.5 * jnp.dot(inv_root, root_iter, precision=highest)
        root_iter = jnp.dot(root_iter, correction, precision=highest)
        inv_root = jnp.dot(correction, inv_root, precision=highest)
    shrink = inv_root / jnp.sqrt(trace_bound)
    mean_weight = jnp.dot(shrink, jnp.dot(shrink, drive_vector, precision=highest), precision=highest)
    weights = math.sqrt(members - 1) * shrink + mean_weight[:, None]
    owned_cells = region[:, :, :, MARGIN_WIDTH:MARGIN_WIDTH + BAND, MARGIN_WIDTH:MARGIN_WIDTH + CLON].reshape(members, -1).astype(jnp.float32)
    cell_mean = lax.optimization_barrier(jnp.mean(owned_cells, axis=0))
    perturb = owned_cells - cell_mean[None, :]
    analysed = cell_mean[None, :] + jnp.dot(weights.T, perturb, precision=highest)
    return analysed.astype(jnp.bfloat16).reshape(members, 3, LEV, BAND, CLON)

def reference(sample_collection, layer_depth, obs_where, observed_values, obs_precision, loc_index, obs_count):
    spin_frequency = coriolis_rate(LAT)[:, None]
    reach = 2 * STEPS
    bordered_thickness_grid = jnp.pad(layer_depth, ((0, 0), (0, 0), (reach, reach)), mode='wrap')
    predicted_solution = lax.map(lambda sample_number: sample_prediction(sample_number, bordered_thickness_grid, spin_frequency), sample_collection)
    bordered_array = jnp.pad(predicted_solution, ((0, 0), (0, 0), (0, 0), (MARGIN_WIDTH, MARGIN_WIDTH), (0, 0)))
    bordered_array = jnp.pad(bordered_array, ((0, 0), (0, 0), (0, 0), (0, 0), (MARGIN_WIDTH, MARGIN_WIDTH)), mode='wrap')
    zero = jnp.zeros((), jnp.int32)

    def analyse_device(device_index):
        band_index = (device_index // N_LON).astype(jnp.int32)
        strip_index = (device_index % N_LON).astype(jnp.int32)
        region = lax.dynamic_slice(bordered_array, (zero, zero, zero, band_index * BAND, strip_index * CLON), (MEMBERS, 3, LEV, BAND + 2 * MARGIN_WIDTH, CLON + 2 * MARGIN_WIDTH))
        return analyse(region, obs_where[band_index, strip_index], observed_values[band_index, strip_index], obs_precision[band_index, strip_index], loc_index[band_index, strip_index], obs_count[band_index, strip_index])
    analysed_blocks = lax.map(analyse_device, jnp.arange(N_MEM * N_LON, dtype=jnp.int32))
    analysed_blocks = analysed_blocks.reshape(N_MEM, N_LON, MEMBERS, 3, LEV, BAND, CLON)
    analysed_blocks = jnp.transpose(analysed_blocks, (2, 3, 4, 0, 5, 1, 6))
    return analysed_blocks.reshape(MEMBERS, 3, LEV, LAT, NLON)
```

```python
import functools
import math

import jax
import jax.numpy as jnp
from jax import lax
from jax.experimental import pallas as pl
from jax.experimental.pallas import tpu as pltpu
from jax.sharding import PartitionSpec as P

STEPS = 2
MARGIN_WIDTH = 4
BAND = 4
NS_ITERS = 5
MESH = pl.DeviceIdType.MESH
HIGHEST = lax.Precision.HIGHEST

time_step = 0.8
inflation = 1.1


def coriolis_rate(count_rows):
    latitude = jnp.arange(count_rows, dtype=jnp.float32)
    return 0.4 * (latitude / (count_rows - 1) - 0.5)


def lat_diff(field):
    bordered_array = jnp.pad(field, [(0, 0)] * (field.ndim - 2) + [(1, 1), (0, 0)])
    return 0.5 * (bordered_array[..., 2:, :] - bordered_array[..., :-2, :])


def lon_diff(field):
    return 0.5 * (field[..., 2:] - field[..., :-2])


def advance(fields, depth_cut, spin_frequency):
    height = fields[..., 0, :, :, :]
    east_wind = fields[..., 1, :, :, :]
    north_wind = fields[..., 2, :, :, :]
    flux_east = depth_cut * east_wind
    flux_north = depth_cut * north_wind
    height_new = height[..., 1:-1] - time_step * (
        lon_diff(flux_east) + lat_diff(flux_north)[..., 1:-1]
    )
    east_new = (
        east_wind[..., 2:-2]
        - time_step * lon_diff(height_new)
        + time_step * spin_frequency * north_wind[..., 2:-2]
    )
    north_new = (
        north_wind[..., 2:-2]
        - time_step * lat_diff(height_new)[..., 1:-1]
        - time_step * spin_frequency * east_wind[..., 2:-2]
    )
    return jnp.stack([height_new[..., 1:-1], east_new, north_new], axis=-4)


def extended_lon(value, width):
    count, length = lax.axis_size("lon"), value.shape[-1]
    up = [(i, (i + 1) % count) for i in range(count)]
    down = [(j, i) for i, j in up]
    before = lax.ppermute(value[..., length - width :], "lon", up)
    after = lax.ppermute(value[..., :width], "lon", down)
    return jnp.concatenate([before, value, after], axis=-1)


def exchange_order(n):
    return sorted(range(1, n), key=lambda d: (-min(d, n - d), d))


def analysis_kernel(
    n, picks_ref, cells_ref, values_ref, weight_ref, out_ref,
    picked, cells, result, transform, pick_send, pick_recv, cell_send, cell_recv, back_send, back_recv,
):
    me = lax.axis_index("mem")
    group = cells_ref.shape[1]
    members = n * group

    barrier = pltpu.get_barrier_semaphore()
    for d in range(1, n):
        pl.semaphore_signal(
            barrier, inc=1, device_id={"mem": lax.rem(me + d, n)}, device_id_type=MESH
        )
    pl.semaphore_wait(barrier, n - 1)

    def send(src, dst, ss, rs, d):
        peer = lax.rem(me + d, n)
        return pltpu.make_async_remote_copy(
            src_ref=src, dst_ref=dst, send_sem=ss.at[d], recv_sem=rs.at[d],
            device_id={"mem": peer}, device_id_type=MESH,
        )

    order = exchange_order(n)
    pick_copies = [
        send(picks_ref.at[d], picked.at[me], pick_send, pick_recv, d) for d in order
    ]
    for copy in pick_copies:
        copy.start()
    cell_copies = [
        send(cells_ref.at[lax.rem(me + d, n)], cells.at[me], cell_send, cell_recv, d)
        for d in order
    ]
    for copy in cell_copies:
        copy.start()
    picked[me] = picks_ref[0]
    cells[me] = cells_ref[me]
    for copy in pick_copies:
        copy.wait()

    obs = picked[...].astype(jnp.float32).reshape(members, -1)
    obs_mean = jnp.mean(obs, axis=0, keepdims=True)
    spread = obs - obs_mean
    weighted = spread * weight_ref[...]
    innovation = values_ref[...] - obs_mean

    def mm(a, b):
        return jnp.dot(a, b, precision=HIGHEST, preferred_element_type=jnp.float32)

    gram = lax.dot_general(
        weighted, spread, (((1,), (1,)), ((), ())),
        precision=HIGHEST, preferred_element_type=jnp.float32,
    )
    drive = jnp.sum(weighted * innovation, axis=1, keepdims=True)
    prior = (members - 1) / inflation
    trace = jnp.sum(jnp.sum(weighted * spread, axis=1, keepdims=True), axis=0, keepdims=True)
    trace_bound = prior + trace
    row_at = lax.broadcasted_iota(jnp.int32, (members, members), 0)
    column_at = lax.broadcasted_iota(jnp.int32, (members, members), 1)
    identity = jnp.where(row_at == column_at, 1.0, 0.0).astype(jnp.float32)
    root_iter = (gram + prior * identity) / trace_bound
    correction = 1.5 * identity - 0.5 * root_iter
    root_iter = mm(root_iter, correction)
    inv_root = correction
    for sweep in range(1, NS_ITERS):
        correction = 1.5 * identity - 0.5 * mm(inv_root, root_iter)
        if sweep < NS_ITERS - 1:
            root_iter = mm(root_iter, correction)
        inv_root = mm(correction, inv_root)
    shrink = inv_root * lax.rsqrt(trace_bound)
    inner = jnp.sum(shrink * drive, axis=0, keepdims=True)
    mean_weight = jnp.sum(shrink * inner, axis=1, keepdims=True)
    weights = math.sqrt(members - 1) * shrink + mean_weight
    weights = weights + (1.0 - jnp.sum(weights, axis=0, keepdims=True)) / members
    weights_t = weights.T
    high = weights_t.astype(jnp.bfloat16)
    transform[0] = high
    transform[1] = (weights_t - high.astype(jnp.float32)).astype(jnp.bfloat16)

    for copy in cell_copies:
        copy.wait()
    all_cells = cells[...].reshape(members, -1)

    def analysed(peer):
        rows = pl.ds(pl.multiple_of(peer * group, group), group)
        total = jnp.dot(transform[0, rows, :], all_cells, preferred_element_type=jnp.float32)
        total += jnp.dot(transform[1, rows, :], all_cells, preferred_element_type=jnp.float32)
        return total.astype(jnp.bfloat16)

    back_copies = []
    for d in order:
        peer = lax.rem(me + d, n)
        result[d] = analysed(peer)
        copy = send(result.at[d], out_ref.at[me], back_send, back_recv, d)
        copy.start()
        back_copies.append(copy)
    out_ref[me] = analysed(me)
    for copy in back_copies:
        copy.wait()


def on_device(
    sample_collection, layer_depth, obs_where, observed_values, obs_precision, loc_index, obs_count
):
    n = lax.axis_size("mem")
    me = lax.axis_index("mem")
    group, _, _, count_rows, strip = sample_collection.shape
    slots = obs_where.shape[-1]
    wheres = [obs_where[0, 0]]
    for d in range(1, n):
        pairs = [((i + d) % n, i) for i in range(n)]
        wheres.append(lax.ppermute(obs_where[0, 0], "mem", pairs))

    spin_frequency = coriolis_rate(count_rows)[:, None]
    reach = 2 * STEPS + MARGIN_WIDTH
    depth = extended_lon(layer_depth, reach)
    fields = extended_lon(sample_collection, reach).astype(jnp.float32)
    for step_index in range(STEPS):
        fields = advance(
            fields, depth[..., 2 * step_index : depth.shape[-1] - 2 * step_index], spin_frequency
        )
    fore = fields.astype(jnp.bfloat16)[:, :, 0]
    own = fore[..., MARGIN_WIDTH : MARGIN_WIDTH + strip]
    cells = own.reshape(group, 3, n, BAND, strip).transpose(2, 0, 1, 3, 4).reshape(n, group, -1)

    padded = jnp.pad(fore, ((0, 0), (0, 0), (MARGIN_WIDTH, MARGIN_WIDTH), (0, 0)))
    tall, wide = count_rows + 2 * MARGIN_WIDTH, strip + 2 * MARGIN_WIDTH
    area = (BAND + 2 * MARGIN_WIDTH) * wide
    flat = padded.reshape(group, -1)
    picks = []
    for d in range(n):
        band = lax.rem(me + d, n)
        component = wheres[d] // area
        at = component * (tall * wide) + band * (BAND * wide) + wheres[d] % area
        picks.append(at)
    picks = jnp.take(flat, jnp.concatenate(picks), axis=1, mode="clip")
    picks = picks.reshape(group, n, slots).transpose(1, 0, 2)

    live_slots = (jnp.arange(slots, dtype=jnp.int32) < obs_count[0, 0]).astype(jnp.float32)
    taper = 1.0 - loc_index[0, 0].astype(jnp.float32) / 16.0
    weight = obs_precision[0, 0] * (taper * taper) * live_slots

    vmem = pl.BlockSpec(memory_space=pltpu.VMEM)
    dma = pltpu.SemaphoreType.DMA
    out = pl.pallas_call(
        functools.partial(analysis_kernel, n),
        out_shape=jax.ShapeDtypeStruct(cells.shape, jnp.bfloat16),
        in_specs=[vmem] * 4,
        out_specs=vmem,
        scratch_shapes=[
            pltpu.VMEM(picks.shape, jnp.bfloat16),
            pltpu.VMEM(cells.shape, jnp.bfloat16),
            pltpu.VMEM(cells.shape, jnp.bfloat16),
            pltpu.VMEM((2, n * group, n * group), jnp.bfloat16),
        ]
        + [dma((n,))] * 6,
        compiler_params=pltpu.CompilerParams(collective_id=0, has_side_effects=True),
    )(picks, cells, observed_values[0], weight[None])
    out = out.reshape(n, group, 3, BAND, strip).transpose(1, 2, 0, 3, 4)
    return out.reshape(sample_collection.shape)


def solution(mesh):
    in_specs = (
        P("mem", None, None, None, "lon"),
        P(None, None, "lon"),
        P("mem", "lon", None),
        P("mem", "lon", None),
        P("mem", "lon", None),
        P("mem", "lon", None),
        P("mem", "lon"),
    )
    out_specs = P("mem", None, None, None, "lon")
    return jax.shard_map(
        on_device, mesh=mesh, in_specs=in_specs, out_specs=out_specs, check_vma=False
    )
```

```python
import functools
import math

import jax
import jax.numpy as jnp
from jax import lax
from jax.experimental import pallas as pl
from jax.experimental.pallas import tpu as pltpu
from jax.sharding import PartitionSpec as P

STEPS = 2
MARGIN_WIDTH = 4
BAND = 4
NS_ITERS = 5
MESH = pl.DeviceIdType.MESH
HIGHEST = lax.Precision.HIGHEST

time_step = 0.8
inflation = 1.1


LANES = 128
REACH = 2 * STEPS + MARGIN_WIDTH
TILE = 16


def coriolis_rate(shape):
    latitude = lax.broadcasted_iota(jnp.int32, shape, 0).astype(jnp.float32)
    return 0.4 * (latitude / (shape[0] - 1) - 0.5)


def lat_diff(field):
    edge = jnp.zeros_like(field[:1])
    north = jnp.concatenate([field[1:], edge], axis=0)
    south = jnp.concatenate([edge, field[:-1]], axis=0)
    return 0.5 * (north - south)


def shifted(field, shift):
    return pltpu.roll(field, shift % LANES, axis=field.ndim - 1)


def lon_diff(field):
    return 0.5 * (shifted(field, -1) - shifted(field, 1))


def forecast(height, east, north, depth, spin):
    for step_index in range(STEPS):
        height_new = height - time_step * (lon_diff(depth * east) + lat_diff(depth * north))
        east_new = east - time_step * lon_diff(height_new) + time_step * spin * north
        north_new = north - time_step * lat_diff(height_new) - time_step * spin * east
        height, east, north = height_new, east_new, north_new
    return height, east, north


def exchange_order(n):
    return sorted(range(1, n), key=lambda d: (-min(d, n - d), d))


def edge_window(own, west, east, lane):
    value = jnp.where(lane < REACH, west, shifted(own, REACH))
    value = jnp.where(lane >= 2 * REACH, shifted(own, 3 * REACH), value)
    return jnp.where((lane >= 3 * REACH) & (lane < 4 * REACH), east, value)


def analysis_kernel(
    n, x_ref, depth_ref, where_ref, values_ref, precision_ref, loc_ref, count_ref, out_ref,
    halo_out, halo_in, depth_in, wheres, main, edge, picks, picked, cells, result, transform,
    halo_send, halo_recv, depth_send, depth_recv, where_send, where_recv,
    pick_send, pick_recv, cell_send, cell_recv, back_send, back_recv,
):
    me = lax.axis_index("mem")
    lon, strips = lax.axis_index("lon"), lax.axis_size("lon")
    right, left = lax.rem(lon + 1, strips), lax.rem(lon + strips - 1, strips)
    _, rows, group, _ = x_ref.shape
    members = n * group
    slots = values_ref.shape[1]
    per_tile = LANES // REACH
    margin = MARGIN_WIDTH

    barrier = pltpu.get_barrier_semaphore()
    for d in range(1, n):
        pl.semaphore_signal(
            barrier, inc=1, device_id={"mem": lax.rem(me + d, n)}, device_id_type=MESH
        )
    for side in (left, right):
        pl.semaphore_signal(barrier, inc=1, device_id={"lon": side}, device_id_type=MESH)

    lane = lax.broadcasted_iota(jnp.int32, (TILE, LANES), 1)

    @pl.loop(0, 3 * (group // TILE))
    def _(at):
        c, m = at // (group // TILE), pl.ds(pl.multiple_of(at % (group // TILE) * TILE, TILE), TILE)
        for k in range(rows // per_tile):
            first = last = jnp.zeros((TILE, LANES), jnp.float32)
            for r in range(per_tile):
                own = x_ref[c, k * per_tile + r, m, :].astype(jnp.float32)
                here = (lane >= r * REACH) & (lane < (r + 1) * REACH)
                first = jnp.where(here, shifted(own, r * REACH), first)
                last = jnp.where(here, shifted(own, (r + 1) * REACH), last)
            halo_out[0, c, k, m, :] = last.astype(jnp.bfloat16)
            halo_out[1, c, k, m, :] = first.astype(jnp.bfloat16)

    pl.semaphore_wait(barrier, n + 1)

    def send(src, dst, ss, rs, i, peer):
        copy = pltpu.make_async_remote_copy(
            src_ref=src, dst_ref=dst, send_sem=ss.at[i], recv_sem=rs.at[i],
            device_id=peer, device_id_type=MESH,
        )
        copy.start()
        return copy

    order = exchange_order(n)
    halo_copies, where_copies = [], []
    for i, side in enumerate((right, left)):
        peer = {"lon": side}
        halo_copies.append(send(halo_out.at[i], halo_in.at[i], halo_send, halo_recv, i, peer))
        halo_copies.append(send(depth_ref, depth_in.at[i], depth_send, depth_recv, i, peer))
    for d in order:
        peer = {"mem": lax.rem(me + d, n)}
        where_copies.append(send(where_ref, wheres.at[me], where_send, where_recv, d, peer))
    wheres[me] = where_ref[...]

    spin = coriolis_rate((rows, 1, LANES))
    blank = jnp.zeros((margin, TILE, LANES), jnp.bfloat16)

    def group_rows(g):
        return pl.ds(pl.multiple_of(g * TILE, TILE), TILE)

    def put(ref, c, m, value):
        ref[c, pl.ds(0, margin), m, :] = blank
        ref[c, pl.ds(margin, rows), m, :] = value
        ref[c, pl.ds(margin + rows, margin), m, :] = blank

    own_depth = depth_ref[...].reshape(rows, 1, LANES)

    @pl.loop(0, group // TILE)
    def _(g):
        m = group_rows(g)
        fields = forecast(
            *[x_ref[c, :, m, :].astype(jnp.float32) for c in range(3)], own_depth, spin
        )
        for c in range(3):
            put(main, c, m, fields[c].astype(jnp.bfloat16))

    for copy in halo_copies:
        copy.wait()

    lane_row = lax.broadcasted_iota(jnp.int32, (rows, LANES), 1)
    edge_depth = edge_window(
        depth_ref[...],
        shifted(depth_in[0], REACH),
        shifted(depth_in[1], 3 * REACH),
        lane_row,
    ).reshape(rows, 1, LANES)

    @pl.loop(0, group // TILE)
    def _(g):
        m = group_rows(g)
        windows = []
        for c in range(3):
            window = []
            for r in range(rows):
                k, slot = r // per_tile, r % per_tile
                own = x_ref[c, r, m, :].astype(jnp.float32)
                west = shifted(halo_in[0, c, k, m, :].astype(jnp.float32), -slot * REACH)
                east = shifted(halo_in[1, c, k, m, :].astype(jnp.float32), (3 - slot) * REACH)
                window.append(edge_window(own, west, east, lane))
            windows.append(jnp.stack(window))
        fields = forecast(*windows, edge_depth, spin)
        for c in range(3):
            value = fields[c].astype(jnp.bfloat16)
            put(edge, c, m, value)
            value = value.astype(jnp.float32)
            inside = main[c, pl.ds(margin, rows), m, :].astype(jnp.float32)
            inside = jnp.where(lane < 2 * STEPS, shifted(value, -REACH), inside)
            inside = jnp.where(
                lane >= LANES - 2 * STEPS, shifted(value, LANES - 3 * REACH), inside
            )
            main[c, pl.ds(margin, rows), m, :] = inside.astype(jnp.bfloat16)

    def send_cells(d):
        to = lax.rem(me + d, n)
        src = main.at[:, pl.ds(margin + to * BAND, BAND)]
        return send(src, cells.at[me], cell_send, cell_recv, d, {"mem": to})

    ahead = len(order) // 3 if n > 3 else 0
    cell_copies = [send_cells(d) for d in order[:ahead]]
    cells[me] = main[:, pl.ds(margin + me * BAND, BAND)]
    for copy in where_copies:
        copy.wait()

    tall = BAND + 2 * margin
    place = lax.broadcasted_iota(jnp.int32, (LANES, slots), 0)

    def pick(band):
        rank, column = wheres[band, 0:1, :], wheres[band, 1:2, :]
        border = jnp.where(column < margin, column + REACH - margin, -1)
        border = jnp.where(
            column >= LANES + margin, column - (LANES + margin) + 3 * REACH, border
        )
        chosen = jnp.concatenate([place == column - margin, place == border], axis=0)
        chosen = jnp.where(chosen, 1.0, 0.0).astype(jnp.bfloat16)
        total = jnp.zeros((group, slots), jnp.float32)
        for c in range(3):
            span = pl.ds(band * BAND, tall)
            area = jnp.concatenate([main[c, span], edge[c, span]], axis=-1)
            at_columns = jnp.dot(
                area.reshape(tall * group, 2 * LANES), chosen, preferred_element_type=jnp.float32
            )
            for r in range(tall):
                part = at_columns[r * group : (r + 1) * group]
                total = jnp.where(rank == c * tall + r, part, total)
        return total.astype(jnp.bfloat16)

    pick_copies = []
    for d in order:
        to = lax.rem(me + d, n)
        picks[d] = pick(to)
        pick_copies.append(
            send(picks.at[d], picked.at[me], pick_send, pick_recv, d, {"mem": to})
        )
    cell_copies += [send_cells(d) for d in order[ahead:]]
    picked[me] = pick(me)
    for copy in pick_copies:
        copy.wait()

    taper = 1.0 - loc_ref[...].astype(jnp.float32) / 16.0
    slot_at = lax.broadcasted_iota(jnp.int32, (1, slots), 1)
    weight = jnp.where(slot_at < count_ref[...], precision_ref[...] * (taper * taper), 0.0)
    obs = picked[...].astype(jnp.float32).reshape(members, slots)
    obs_mean = jnp.mean(obs, axis=0, keepdims=True)
    spread = obs - obs_mean
    weighted = spread * weight
    innovation = values_ref[...] - obs_mean

    def mm(a, b):
        return jnp.dot(a, b, precision=HIGHEST, preferred_element_type=jnp.float32)

    gram = lax.dot_general(
        weighted, spread, (((1,), (1,)), ((), ())),
        precision=HIGHEST, preferred_element_type=jnp.float32,
    )
    drive = jnp.sum(weighted * innovation, axis=1, keepdims=True)
    prior = (members - 1) / inflation
    trace = jnp.sum(jnp.sum(weighted * spread, axis=1, keepdims=True), axis=0, keepdims=True)
    trace_bound = prior + trace
    row_at = lax.broadcasted_iota(jnp.int32, (members, members), 0)
    column_at = lax.broadcasted_iota(jnp.int32, (members, members), 1)
    identity = jnp.where(row_at == column_at, 1.0, 0.0).astype(jnp.float32)
    root_iter = (gram + prior * identity) / trace_bound
    correction = 1.5 * identity - 0.5 * root_iter
    root_iter = mm(root_iter, correction)
    inv_root = correction
    for sweep in range(1, NS_ITERS):
        correction = 1.5 * identity - 0.5 * mm(inv_root, root_iter)
        if sweep < NS_ITERS - 1:
            root_iter = mm(root_iter, correction)
        inv_root = mm(correction, inv_root)
    shrink = inv_root * lax.rsqrt(trace_bound)
    inner = jnp.sum(shrink * drive, axis=0, keepdims=True)
    mean_weight = jnp.sum(shrink * inner, axis=1, keepdims=True)
    weights = math.sqrt(members - 1) * shrink + mean_weight
    weights = weights + (1.0 - jnp.sum(weights, axis=0, keepdims=True)) / members
    weights_t = weights.T
    high = weights_t.astype(jnp.bfloat16)
    transform[0] = high
    transform[1] = (weights_t - high.astype(jnp.float32)).astype(jnp.bfloat16)

    for copy in cell_copies:
        copy.wait()
    all_cells = jnp.concatenate(
        [cells[:, c, r].reshape(members, LANES) for c in range(3) for r in range(BAND)], axis=1
    )

    def analysed(peer):
        rows = pl.ds(pl.multiple_of(peer * group, group), group)
        total = jnp.dot(transform[0, rows, :], all_cells, preferred_element_type=jnp.float32)
        total += jnp.dot(transform[1, rows, :], all_cells, preferred_element_type=jnp.float32)
        return total.astype(jnp.bfloat16)

    def store(ref, at, value):
        for c in range(3):
            for r in range(BAND):
                start = (c * BAND + r) * LANES
                ref[at, c, r] = value[:, start : start + LANES]

    back_copies = []
    for d in order:
        peer = lax.rem(me + d, n)
        store(result, d, analysed(peer))
        back_copies.append(
            send(result.at[d], out_ref.at[me], back_send, back_recv, d, {"mem": peer})
        )
    store(out_ref, me, analysed(me))
    for copy in back_copies:
        copy.wait()


def on_device(
    sample_collection, layer_depth, obs_where, observed_values, obs_precision, loc_index, obs_count
):
    n = lax.axis_size("mem")
    group, _, _, rows, strip = sample_collection.shape
    slots = obs_where.shape[-1]
    wide = strip + 2 * MARGIN_WIDTH
    x = sample_collection[:, :, 0].transpose(1, 2, 0, 3)
    where = jnp.stack([obs_where[0, 0] // wide, obs_where[0, 0] % wide])
    vmem = pl.BlockSpec(memory_space=pltpu.VMEM)
    dma = pltpu.SemaphoreType.DMA
    bf16 = jnp.bfloat16
    halo = (2, 3, rows // (LANES // REACH), group, LANES)
    padded = (3, rows + 2 * MARGIN_WIDTH, group, LANES)
    block = (n, 3, BAND, group, LANES)
    out = pl.pallas_call(
        functools.partial(analysis_kernel, n),
        out_shape=jax.ShapeDtypeStruct(block, bf16),
        in_specs=[vmem] * 7,
        out_specs=vmem,
        scratch_shapes=[
            pltpu.VMEM(halo, bf16),
            pltpu.VMEM(halo, bf16),
            pltpu.VMEM((2, rows, LANES), jnp.float32),
            pltpu.VMEM((n, 2, slots), jnp.int32),
            pltpu.VMEM(padded, bf16),
            pltpu.VMEM(padded, bf16),
            pltpu.VMEM((n, group, slots), bf16),
            pltpu.VMEM((n, group, slots), bf16),
            pltpu.VMEM(block, bf16),
            pltpu.VMEM(block, bf16),
            pltpu.VMEM((2, n * group, n * group), bf16),
        ]
        + [dma((2,))] * 4
        + [dma((n,))] * 8,
        compiler_params=pltpu.CompilerParams(collective_id=0, has_side_effects=True),
    )(x, layer_depth[0], where, observed_values[0], obs_precision[0], loc_index[0], obs_count)
    out = out.transpose(3, 1, 0, 2, 4)
    return out.reshape(sample_collection.shape)


def solution(mesh):
    in_specs = (
        P("mem", None, None, None, "lon"),
        P(None, None, "lon"),
        P("mem", "lon", None),
        P("mem", "lon", None),
        P("mem", "lon", None),
        P("mem", "lon", None),
        P("mem", "lon"),
    )
    out_specs = P("mem", None, None, None, "lon")
    return jax.shard_map(
        on_device, mesh=mesh, in_specs=in_specs, out_specs=out_specs, check_vma=False
    )
```

```python
import functools
import math

import jax
import jax.numpy as jnp
from jax import lax
from jax.experimental import pallas as pl
from jax.experimental.pallas import tpu as pltpu
from jax.sharding import PartitionSpec as P

STEPS = 2
MARGIN_WIDTH = 4
BAND = 4
NS_ITERS = 5
MESH = pl.DeviceIdType.MESH
HIGHEST = lax.Precision.HIGHEST

time_step = 0.8
inflation = 1.1


LANES = 128
REACH = 2 * STEPS + MARGIN_WIDTH
TILE = 16


def coriolis_rate(shape):
    latitude = lax.broadcasted_iota(jnp.int32, shape, 0).astype(jnp.float32)
    return 0.4 * (latitude / (shape[0] - 1) - 0.5)


def lat_diff(field):
    edge = jnp.zeros_like(field[:1])
    north = jnp.concatenate([field[1:], edge], axis=0)
    south = jnp.concatenate([edge, field[:-1]], axis=0)
    return 0.5 * (north - south)


def shifted(field, shift):
    return pltpu.roll(field, shift % LANES, axis=field.ndim - 1)


def lon_diff(field):
    return 0.5 * (shifted(field, -1) - shifted(field, 1))


def forecast(height, east, north, depth, spin):
    for step_index in range(STEPS):
        height_new = height - time_step * (lon_diff(depth * east) + lat_diff(depth * north))
        east_new = east - time_step * lon_diff(height_new) + time_step * spin * north
        north_new = north - time_step * lat_diff(height_new) - time_step * spin * east
        height, east, north = height_new, east_new, north_new
    return height, east, north


def exchange_order(n):
    return sorted(range(1, n), key=lambda d: (-min(d, n - d), d))


def edge_window(own, west, east, lane):
    value = jnp.where(lane < REACH, west, shifted(own, REACH))
    value = jnp.where(lane >= 2 * REACH, shifted(own, 3 * REACH), value)
    return jnp.where((lane >= 3 * REACH) & (lane < 4 * REACH), east, value)


def analysis_kernel(
    n, x_ref, depth_ref, where_ref, values_ref, precision_ref, loc_ref, count_ref, out_ref,
    halo_out, halo_in, depth_in, wheres, main, fixed, edge, border_out, border_in, picks, picked, cells, result, transform,
    halo_send, halo_recv, depth_send, depth_recv, where_send, where_recv,
    border_send, border_recv, pick_send, pick_recv, cell_send, cell_recv, back_send, back_recv,
):
    me = lax.axis_index("mem")
    lon, strips = lax.axis_index("lon"), lax.axis_size("lon")
    right, left = lax.rem(lon + 1, strips), lax.rem(lon + strips - 1, strips)
    _, rows, group, _ = x_ref.shape
    members = n * group
    slots = values_ref.shape[1]
    per_tile = LANES // REACH
    margin = MARGIN_WIDTH

    barrier = pltpu.get_barrier_semaphore()
    for d in range(1, n):
        pl.semaphore_signal(
            barrier, inc=1, device_id={"mem": lax.rem(me + d, n)}, device_id_type=MESH
        )
    for side in (left, right):
        pl.semaphore_signal(barrier, inc=1, device_id={"lon": side}, device_id_type=MESH)

    lane = lax.broadcasted_iota(jnp.int32, (TILE, LANES), 1)

    @pl.loop(0, 3 * (group // TILE))
    def _(at):
        c, m = at // (group // TILE), pl.ds(pl.multiple_of(at % (group // TILE) * TILE, TILE), TILE)
        for k in range(rows // per_tile):
            first = last = jnp.zeros((TILE, LANES), jnp.float32)
            for r in range(per_tile):
                own = x_ref[c, k * per_tile + r, m, :].astype(jnp.float32)
                here = (lane >= r * REACH) & (lane < (r + 1) * REACH)
                first = jnp.where(here, shifted(own, r * REACH), first)
                last = jnp.where(here, shifted(own, (r + 1) * REACH), last)
            halo_out[0, c, k, m, :] = last.astype(jnp.bfloat16)
            halo_out[1, c, k, m, :] = first.astype(jnp.bfloat16)

    spin = coriolis_rate((rows, 1, LANES))
    blank = jnp.zeros((margin, TILE, LANES), jnp.bfloat16)

    def group_rows(g):
        return pl.ds(pl.multiple_of(g * TILE, TILE), TILE)

    def put(ref, c, m, value):
        ref[c, pl.ds(0, margin), m, :] = blank
        ref[c, pl.ds(margin, rows), m, :] = value
        ref[c, pl.ds(margin + rows, margin), m, :] = blank

    own_depth = depth_ref[...].reshape(rows, 1, LANES)

    @pl.loop(0, group // TILE)
    def _(g):
        m = group_rows(g)
        fields = forecast(
            *[x_ref[c, :, m, :].astype(jnp.float32) for c in range(3)], own_depth, spin
        )
        for c in range(3):
            main[c, :, m, :] = fields[c].astype(jnp.bfloat16)

    pl.semaphore_wait(barrier, n + 1)

    def send(src, dst, ss, rs, i, peer):
        copy = pltpu.make_async_remote_copy(
            src_ref=src, dst_ref=dst, send_sem=ss.at[i], recv_sem=rs.at[i],
            device_id=peer, device_id_type=MESH,
        )
        copy.start()
        return copy

    order = exchange_order(n)
    halo_copies, where_copies = [], []
    for i, side in enumerate((right, left)):
        peer = {"lon": side}
        halo_copies.append(send(halo_out.at[i], halo_in.at[i], halo_send, halo_recv, i, peer))
        halo_copies.append(send(depth_ref, depth_in.at[i], depth_send, depth_recv, i, peer))
    for d in order:
        peer = {"mem": lax.rem(me + d, n)}
        where_copies.append(send(where_ref, wheres.at[me], where_send, where_recv, d, peer))
    wheres[me] = where_ref[...]

    def send_cells(d, ref, skip):
        to = lax.rem(me + d, n)
        src = ref.at[:, pl.ds(to * BAND + skip, BAND)]
        return send(src, cells.at[me], cell_send, cell_recv, d, {"mem": to})

    early, late = order[:-1], order[-1:]
    cell_copies = [send_cells(d, main, 0) for d in early]

    for copy in halo_copies:
        copy.wait()

    lane_row = lax.broadcasted_iota(jnp.int32, (rows, LANES), 1)
    edge_depth = edge_window(
        depth_ref[...],
        shifted(depth_in[0], REACH),
        shifted(depth_in[1], 3 * REACH),
        lane_row,
    ).reshape(rows, 1, LANES)

    @pl.loop(0, group // TILE)
    def _(g):
        m = group_rows(g)
        windows = []
        for c in range(3):
            window = []
            for r in range(rows):
                k, slot = r // per_tile, r % per_tile
                own = x_ref[c, r, m, :].astype(jnp.float32)
                west = shifted(halo_in[0, c, k, m, :].astype(jnp.float32), -slot * REACH)
                east = shifted(halo_in[1, c, k, m, :].astype(jnp.float32), (3 - slot) * REACH)
                window.append(edge_window(own, west, east, lane))
            windows.append(jnp.stack(window))
        fields = forecast(*windows, edge_depth, spin)
        for c in range(3):
            value = fields[c].astype(jnp.bfloat16)
            put(edge, c, m, value)
            value = value.astype(jnp.float32)
            inside = main[c, :, m, :].astype(jnp.float32)
            inside = jnp.where(lane < 2 * STEPS, shifted(value, -REACH), inside)
            inside = jnp.where(
                lane >= LANES - 2 * STEPS, shifted(value, LANES - 3 * REACH), inside
            )
            put(fixed, c, m, inside.astype(jnp.bfloat16))

    cells[me] = fixed[:, pl.ds(margin + me * BAND, BAND)]

    @pl.loop(0, group // TILE)
    def _(g):
        m = group_rows(g)
        for i, d in enumerate(early):
            to = lax.rem(me + d, n)
            packed = jnp.zeros((TILE, LANES), jnp.float32)
            for c in range(3):
                for r in range(BAND):
                    start = (c * BAND + r) * REACH
                    part = edge[c, margin + to * BAND + r, m, :].astype(jnp.float32)
                    west = (lane >= start) & (lane < start + 2 * STEPS)
                    east = (lane >= start + 2 * STEPS) & (lane < start + REACH)
                    packed = jnp.where(west, shifted(part, start - REACH), packed)
                    moved = shifted(part, start + 4 * STEPS - 3 * REACH)
                    packed = jnp.where(east, moved, packed)
            border_out[i, m, :] = packed.astype(jnp.bfloat16)

    border_copies = [
        send(border_out.at[i], border_in.at[i], border_send, border_recv, i,
             {"mem": lax.rem(me + d, n)})
        for i, d in enumerate(early)
    ]
    for copy in where_copies:
        copy.wait()

    tall = BAND + 2 * margin
    place = lax.broadcasted_iota(jnp.int32, (LANES, slots), 0)

    def pick(band):
        where = wheres[band].astype(jnp.float32)
        rank = jnp.floor((where + 0.5) * (1.0 / (LANES + 2 * margin)))
        column = (where - rank * (LANES + 2 * margin)).astype(jnp.int32)
        border = jnp.where(column < margin, column + REACH - margin, -1)
        border = jnp.where(
            column >= LANES + margin, column - (LANES + margin) + 3 * REACH, border
        )
        chosen = jnp.concatenate([place == column - margin, place == border], axis=0)
        chosen = jnp.where(chosen, 1.0, 0.0).astype(jnp.bfloat16)
        total = jnp.zeros((group, slots), jnp.float32)
        for c in range(3):
            span = pl.ds(band * BAND, tall)
            area = jnp.concatenate([fixed[c, span], edge[c, span]], axis=-1)
            at_columns = jnp.dot(
                area.reshape(tall * group, 2 * LANES), chosen, preferred_element_type=jnp.float32
            )
            for r in range(tall):
                part = at_columns[r * group : (r + 1) * group]
                total = jnp.where(rank == float(c * tall + r), part, total)
        return total.astype(jnp.bfloat16)

    pick_copies = []
    for d in order:
        to = lax.rem(me + d, n)
        picks[d] = pick(to)
        pick_copies.append(
            send(picks.at[d], picked.at[me], pick_send, pick_recv, d, {"mem": to})
        )
    late_copies = [send_cells(d, fixed, margin) for d in late]
    picked[me] = pick(me)
    for copy in cell_copies + border_copies:
        copy.wait()

    @pl.loop(0, group // TILE)
    def _(g):
        m = group_rows(g)
        for i, d in enumerate(early):
            source = lax.rem(me + n - d, n)
            packed = border_in[i, m, :].astype(jnp.float32)
            for c in range(3):
                for r in range(BAND):
                    start = (c * BAND + r) * REACH
                    value = cells[source, c, r, m, :].astype(jnp.float32)
                    value = jnp.where(lane < 2 * STEPS, shifted(packed, -start), value)
                    moved = shifted(packed, LANES - start - 4 * STEPS)
                    value = jnp.where(lane >= LANES - 2 * STEPS, moved, value)
                    cells[source, c, r, m, :] = value.astype(jnp.bfloat16)

    for copy in pick_copies:
        copy.wait()

    taper = 1.0 - loc_ref[...].astype(jnp.float32) / 16.0
    slot_at = lax.broadcasted_iota(jnp.int32, (1, slots), 1)
    weight = jnp.where(slot_at < count_ref[...], precision_ref[...] * (taper * taper), 0.0)
    obs = picked[...].astype(jnp.float32).reshape(members, slots)
    obs_mean = jnp.mean(obs, axis=0, keepdims=True)
    spread = obs - obs_mean
    weighted = spread * weight
    innovation = values_ref[...] - obs_mean

    def mm(a, b):
        return jnp.dot(a, b, precision=HIGHEST, preferred_element_type=jnp.float32)

    gram = lax.dot_general(
        weighted, spread, (((1,), (1,)), ((), ())),
        precision=HIGHEST, preferred_element_type=jnp.float32,
    )
    drive = jnp.sum(weighted * innovation, axis=1, keepdims=True)
    prior = (members - 1) / inflation
    trace = jnp.sum(jnp.sum(weighted * spread, axis=1, keepdims=True), axis=0, keepdims=True)
    trace_bound = prior + trace
    row_at = lax.broadcasted_iota(jnp.int32, (members, members), 0)
    column_at = lax.broadcasted_iota(jnp.int32, (members, members), 1)
    identity = jnp.where(row_at == column_at, 1.0, 0.0).astype(jnp.float32)
    root_iter = (gram + prior * identity) / trace_bound
    correction = 1.5 * identity - 0.5 * root_iter
    root_iter = mm(root_iter, correction)
    inv_root = correction
    for sweep in range(1, NS_ITERS):
        correction = 1.5 * identity - 0.5 * mm(inv_root, root_iter)
        if sweep < NS_ITERS - 1:
            root_iter = mm(root_iter, correction)
        inv_root = mm(correction, inv_root)
    shrink = inv_root * lax.rsqrt(trace_bound)
    inner = jnp.sum(shrink * drive, axis=0, keepdims=True)
    mean_weight = jnp.sum(shrink * inner, axis=1, keepdims=True)
    weights = math.sqrt(members - 1) * shrink + mean_weight
    weights = weights + (1.0 - jnp.sum(weights, axis=0, keepdims=True)) / members
    weights_t = weights.T
    high = weights_t.astype(jnp.bfloat16)
    transform[0] = high
    transform[1] = (weights_t - high.astype(jnp.float32)).astype(jnp.bfloat16)

    for copy in late_copies:
        copy.wait()
    all_cells = jnp.concatenate(
        [cells[:, c, r].reshape(members, LANES) for c in range(3) for r in range(BAND)], axis=1
    )

    def analysed(peer):
        rows = pl.ds(pl.multiple_of(peer * group, group), group)
        total = jnp.dot(transform[0, rows, :], all_cells, preferred_element_type=jnp.float32)
        total += jnp.dot(transform[1, rows, :], all_cells, preferred_element_type=jnp.float32)
        return total.astype(jnp.bfloat16)

    def slabs(value):
        for c in range(3):
            for r in range(BAND):
                start = (c * BAND + r) * LANES
                yield c, r, value[:, start : start + LANES]

    back_copies = []
    for d in order:
        peer = lax.rem(me + d, n)
        for c, r, value in slabs(analysed(peer)):
            result[d, c, r] = value
        back_copies.append(
            send(result.at[d], out_ref.at[:, pl.ds(me * BAND, BAND)], back_send, back_recv, d, {"mem": peer})
        )
    for c, r, value in slabs(analysed(me)):
        out_ref[c, me * BAND + r] = value
    for copy in back_copies:
        copy.wait()


def on_device(
    sample_collection, layer_depth, obs_where, observed_values, obs_precision, loc_index, obs_count
):
    n = lax.axis_size("mem")
    group, _, _, rows, strip = sample_collection.shape
    slots = obs_where.shape[-1]
    x = sample_collection[:, :, 0].transpose(1, 2, 0, 3)
    vmem = pl.BlockSpec(memory_space=pltpu.VMEM)
    dma = pltpu.SemaphoreType.DMA
    bf16 = jnp.bfloat16
    halo = (2, 3, rows // (LANES // REACH), group, LANES)
    padded = (3, rows + 2 * MARGIN_WIDTH, group, LANES)
    block = (n, 3, BAND, group, LANES)
    out = pl.pallas_call(
        functools.partial(analysis_kernel, n),
        out_shape=jax.ShapeDtypeStruct((3, rows, group, LANES), bf16),
        in_specs=[vmem] * 7,
        out_specs=vmem,
        scratch_shapes=[
            pltpu.VMEM(halo, bf16),
            pltpu.VMEM(halo, bf16),
            pltpu.VMEM((2, rows, LANES), jnp.float32),
            pltpu.VMEM((n, 1, slots), jnp.int32),
            pltpu.VMEM((3, rows, group, LANES), bf16),
            pltpu.VMEM(padded, bf16),
            pltpu.VMEM(padded, bf16),
            pltpu.VMEM((n, group, LANES), bf16),
            pltpu.VMEM((n, group, LANES), bf16),
            pltpu.VMEM((n, group, slots), bf16),
            pltpu.VMEM((n, group, slots), bf16),
            pltpu.VMEM(block, bf16),
            pltpu.VMEM(block, bf16),
            pltpu.VMEM((2, n * group, n * group), bf16),
        ]
        + [dma((2,))] * 4
        + [dma((n,))] * 10,
        compiler_params=pltpu.CompilerParams(collective_id=0, has_side_effects=True),
    )(x, layer_depth[0], obs_where[0], observed_values[0], obs_precision[0], loc_index[0], obs_count)
    out = out.transpose(2, 0, 1, 3)
    return out.reshape(sample_collection.shape)


def solution(mesh):
    in_specs = (
        P("mem", None, None, None, "lon"),
        P(None, None, "lon"),
        P("mem", "lon", None),
        P("mem", "lon", None),
        P("mem", "lon", None),
        P("mem", "lon", None),
        P("mem", "lon"),
    )
    out_specs = P("mem", None, None, None, "lon")
    return jax.shard_map(
        on_device, mesh=mesh, in_specs=in_specs, out_specs=out_specs, check_vma=False
    )
```

```python
import functools
import math

import jax
import jax.numpy as jnp
from jax import lax
from jax.experimental import pallas as pl
from jax.experimental.pallas import tpu as pltpu
from jax.sharding import PartitionSpec as P

STEPS = 2
MARGIN_WIDTH = 4
BAND = 4
NS_ITERS = 5
MESH = pl.DeviceIdType.MESH
HIGHEST = lax.Precision.HIGHEST

time_step = 0.8
inflation = 1.1


LANES = 128
REACH = 2 * STEPS + MARGIN_WIDTH
TILE = 16


def coriolis_rate(shape):
    latitude = lax.broadcasted_iota(jnp.int32, shape, 0).astype(jnp.float32)
    return 0.4 * (latitude / (shape[0] - 1) - 0.5)


def lat_diff(field):
    edge = jnp.zeros_like(field[:1])
    north = jnp.concatenate([field[1:], edge], axis=0)
    south = jnp.concatenate([edge, field[:-1]], axis=0)
    return 0.5 * (north - south)


def shifted(field, shift):
    return pltpu.roll(field, shift % LANES, axis=field.ndim - 1)


def lon_diff(field):
    return 0.5 * (shifted(field, -1) - shifted(field, 1))


def forecast(height, east, north, depth, spin):
    for step_index in range(STEPS):
        height_new = height - time_step * (lon_diff(depth * east) + lat_diff(depth * north))
        east_new = east - time_step * lon_diff(height_new) + time_step * spin * north
        north_new = north - time_step * lat_diff(height_new) - time_step * spin * east
        height, east, north = height_new, east_new, north_new
    return height, east, north


def exchange_order(n):
    return sorted(range(1, n), key=lambda d: (-min(d, n - d), d))


def edge_window(own, west, east, lane):
    value = jnp.where(lane < REACH, west, shifted(own, REACH))
    value = jnp.where(lane >= 2 * REACH, shifted(own, 3 * REACH), value)
    return jnp.where((lane >= 3 * REACH) & (lane < 4 * REACH), east, value)


def analysis_kernel(
    n, x_ref, depth_ref, where_ref, values_ref, precision_ref, loc_ref, count_ref, out_ref,
    halo_out, halo_in, depth_in, wheres, main, fixed, edge, border_out, border_in, picks, picked, cells, result, transform,
    halo_send, halo_recv, depth_send, depth_recv, where_send, where_recv,
    border_send, border_recv, pick_send, pick_recv, cell_send, cell_recv, back_send, back_recv,
):
    me = lax.axis_index("mem")
    lon, strips = lax.axis_index("lon"), lax.axis_size("lon")
    right, left = lax.rem(lon + 1, strips), lax.rem(lon + strips - 1, strips)
    _, rows, group, _ = x_ref.shape
    members = n * group
    slots = values_ref.shape[1]
    per_tile = LANES // REACH
    margin = MARGIN_WIDTH

    barrier = pltpu.get_barrier_semaphore()
    for d in range(1, n):
        pl.semaphore_signal(
            barrier, inc=1, device_id={"mem": lax.rem(me + d, n)}, device_id_type=MESH
        )
    for side in (left, right):
        pl.semaphore_signal(barrier, inc=1, device_id={"lon": side}, device_id_type=MESH)

    lane = lax.broadcasted_iota(jnp.int32, (TILE, LANES), 1)

    @pl.loop(0, 3 * (group // TILE))
    def _(at):
        c, m = at // (group // TILE), pl.ds(pl.multiple_of(at % (group // TILE) * TILE, TILE), TILE)
        for k in range(rows // per_tile):
            first = last = jnp.zeros((TILE, LANES), jnp.float32)
            for r in range(per_tile):
                own = x_ref[c, k * per_tile + r, m, :].astype(jnp.float32)
                here = (lane >= r * REACH) & (lane < (r + 1) * REACH)
                first = jnp.where(here, shifted(own, r * REACH), first)
                last = jnp.where(here, shifted(own, (r + 1) * REACH), last)
            halo_out[0, c, k, m, :] = last.astype(jnp.bfloat16)
            halo_out[1, c, k, m, :] = first.astype(jnp.bfloat16)

    spin = coriolis_rate((rows, 1, LANES))
    blank = jnp.zeros((margin, TILE, LANES), jnp.bfloat16)

    def group_rows(g):
        return pl.ds(pl.multiple_of(g * TILE, TILE), TILE)

    def put(ref, c, m, value):
        ref[c, pl.ds(0, margin), m, :] = blank
        ref[c, pl.ds(margin, rows), m, :] = value
        ref[c, pl.ds(margin + rows, margin), m, :] = blank

    own_depth = depth_ref[...].reshape(rows, 1, LANES)

    @pl.loop(0, group // TILE)
    def _(g):
        m = group_rows(g)
        fields = forecast(
            *[x_ref[c, :, m, :].astype(jnp.float32) for c in range(3)], own_depth, spin
        )
        for c in range(3):
            main[c, :, m, :] = fields[c].astype(jnp.bfloat16)

    pl.semaphore_wait(barrier, n + 1)

    def send(src, dst, ss, rs, i, peer):
        copy = pltpu.make_async_remote_copy(
            src_ref=src, dst_ref=dst, send_sem=ss.at[i], recv_sem=rs.at[i],
            device_id=peer, device_id_type=MESH,
        )
        copy.start()
        return copy

    order = exchange_order(n)
    halo_copies, where_copies = [], []
    for i, side in enumerate((right, left)):
        peer = {"lon": side}
        halo_copies.append(send(halo_out.at[i], halo_in.at[i], halo_send, halo_recv, i, peer))
        halo_copies.append(send(depth_ref, depth_in.at[i], depth_send, depth_recv, i, peer))
    for d in order:
        peer = {"mem": lax.rem(me + d, n)}
        where_copies.append(send(where_ref, wheres.at[me], where_send, where_recv, d, peer))
    wheres[me] = where_ref[...]

    def send_cells(d, ref, skip):
        to = lax.rem(me + d, n)
        src = ref.at[:, pl.ds(to * BAND + skip, BAND)]
        return send(src, cells.at[me], cell_send, cell_recv, d, {"mem": to})

    early, late = order[:-2], order[-2:]
    cell_copies = [send_cells(d, main, 0) for d in early]

    for copy in halo_copies:
        copy.wait()

    lane_row = lax.broadcasted_iota(jnp.int32, (rows, LANES), 1)
    edge_depth = edge_window(
        depth_ref[...],
        shifted(depth_in[0], REACH),
        shifted(depth_in[1], 3 * REACH),
        lane_row,
    ).reshape(rows, 1, LANES)

    @pl.loop(0, group // TILE)
    def _(g):
        m = group_rows(g)
        windows = []
        for c in range(3):
            window = []
            for r in range(rows):
                k, slot = r // per_tile, r % per_tile
                own = x_ref[c, r, m, :].astype(jnp.float32)
                west = shifted(halo_in[0, c, k, m, :].astype(jnp.float32), -slot * REACH)
                east = shifted(halo_in[1, c, k, m, :].astype(jnp.float32), (3 - slot) * REACH)
                window.append(edge_window(own, west, east, lane))
            windows.append(jnp.stack(window))
        fields = forecast(*windows, edge_depth, spin)
        for c in range(3):
            value = fields[c].astype(jnp.bfloat16)
            put(edge, c, m, value)
            value = value.astype(jnp.float32)
            inside = main[c, :, m, :].astype(jnp.float32)
            inside = jnp.where(lane < 2 * STEPS, shifted(value, -REACH), inside)
            inside = jnp.where(
                lane >= LANES - 2 * STEPS, shifted(value, LANES - 3 * REACH), inside
            )
            put(fixed, c, m, inside.astype(jnp.bfloat16))

    cells[me] = fixed[:, pl.ds(margin + me * BAND, BAND)]

    @pl.loop(0, group // TILE)
    def _(g):
        m = group_rows(g)
        for i, d in enumerate(early):
            to = lax.rem(me + d, n)
            packed = jnp.zeros((TILE, LANES), jnp.float32)
            for c in range(3):
                for r in range(BAND):
                    start = (c * BAND + r) * REACH
                    part = edge[c, margin + to * BAND + r, m, :].astype(jnp.float32)
                    west = (lane >= start) & (lane < start + 2 * STEPS)
                    east = (lane >= start + 2 * STEPS) & (lane < start + REACH)
                    packed = jnp.where(west, shifted(part, start - REACH), packed)
                    moved = shifted(part, start + 4 * STEPS - 3 * REACH)
                    packed = jnp.where(east, moved, packed)
            border_out[i, m, :] = packed.astype(jnp.bfloat16)

    border_copies = [
        send(border_out.at[i], border_in.at[i], border_send, border_recv, i,
             {"mem": lax.rem(me + d, n)})
        for i, d in enumerate(early)
    ]
    for copy in where_copies:
        copy.wait()

    tall = BAND + 2 * margin
    place = lax.broadcasted_iota(jnp.int32, (LANES, slots), 0)

    def pick(band):
        where = wheres[band].astype(jnp.float32)
        rank = jnp.floor((where + 0.5) * (1.0 / (LANES + 2 * margin)))
        column = (where - rank * (LANES + 2 * margin)).astype(jnp.int32)
        border = jnp.where(column < margin, column + REACH - margin, -1)
        border = jnp.where(
            column >= LANES + margin, column - (LANES + margin) + 3 * REACH, border
        )
        chosen = jnp.concatenate([place == column - margin, place == border], axis=0)
        chosen = jnp.where(chosen, 1.0, 0.0).astype(jnp.bfloat16)
        total = jnp.zeros((group, slots), jnp.float32)
        for c in range(3):
            span = pl.ds(band * BAND, tall)
            area = jnp.concatenate([fixed[c, span], edge[c, span]], axis=-1)
            at_columns = jnp.dot(
                area.reshape(tall * group, 2 * LANES), chosen, preferred_element_type=jnp.float32
            )
            for r in range(tall):
                part = at_columns[r * group : (r + 1) * group]
                total = jnp.where(rank == float(c * tall + r), part, total)
        return total.astype(jnp.bfloat16)

    pick_copies = []
    for d in order:
        to = lax.rem(me + d, n)
        picks[d] = pick(to)
        pick_copies.append(
            send(picks.at[d], picked.at[me], pick_send, pick_recv, d, {"mem": to})
        )
    late_copies = [send_cells(d, fixed, margin) for d in late]
    picked[me] = pick(me)
    for copy in cell_copies + border_copies:
        copy.wait()

    @pl.loop(0, group // TILE)
    def _(g):
        m = group_rows(g)
        for i, d in enumerate(early):
            source = lax.rem(me + n - d, n)
            packed = border_in[i, m, :].astype(jnp.float32)
            for c in range(3):
                for r in range(BAND):
                    start = (c * BAND + r) * REACH
                    value = cells[source, c, r, m, :].astype(jnp.float32)
                    value = jnp.where(lane < 2 * STEPS, shifted(packed, -start), value)
                    moved = shifted(packed, LANES - start - 4 * STEPS)
                    value = jnp.where(lane >= LANES - 2 * STEPS, moved, value)
                    cells[source, c, r, m, :] = value.astype(jnp.bfloat16)

    for copy in pick_copies:
        copy.wait()

    taper = 1.0 - loc_ref[...].astype(jnp.float32) / 16.0
    slot_at = lax.broadcasted_iota(jnp.int32, (1, slots), 1)
    weight = jnp.where(slot_at < count_ref[...], precision_ref[...] * (taper * taper), 0.0)
    obs = picked[...].astype(jnp.float32).reshape(members, slots)
    obs_mean = jnp.mean(obs, axis=0, keepdims=True)
    spread = obs - obs_mean
    weighted = spread * weight
    innovation = values_ref[...] - obs_mean

    def split(a):
        high = a.astype(jnp.bfloat16)
        return high, (a - high.astype(jnp.float32)).astype(jnp.bfloat16)

    def mm(a, b):
        (ah, al), (bh, bl) = split(a), split(b)
        total = jnp.dot(ah, bl, preferred_element_type=jnp.float32)
        total += jnp.dot(al, bh, preferred_element_type=jnp.float32)
        return total + jnp.dot(ah, bh, preferred_element_type=jnp.float32)

    gram = lax.dot_general(
        weighted, spread, (((1,), (1,)), ((), ())),
        precision=HIGHEST, preferred_element_type=jnp.float32,
    )
    drive = jnp.sum(weighted * innovation, axis=1, keepdims=True)
    prior = (members - 1) / inflation
    trace = jnp.sum(jnp.sum(weighted * spread, axis=1, keepdims=True), axis=0, keepdims=True)
    trace_bound = prior + trace
    row_at = lax.broadcasted_iota(jnp.int32, (members, members), 0)
    column_at = lax.broadcasted_iota(jnp.int32, (members, members), 1)
    identity = jnp.where(row_at == column_at, 1.0, 0.0).astype(jnp.float32)
    root_iter = (gram + prior * identity) / trace_bound
    correction = 1.5 * identity - 0.5 * root_iter
    root_iter = mm(root_iter, correction)
    inv_root = correction
    for sweep in range(1, NS_ITERS):
        correction = 1.5 * identity - 0.5 * mm(inv_root, root_iter)
        if sweep < NS_ITERS - 1:
            root_iter = mm(root_iter, correction)
        inv_root = mm(correction, inv_root)
    shrink = inv_root * lax.rsqrt(trace_bound)
    inner = jnp.sum(shrink * drive, axis=0, keepdims=True)
    mean_weight = jnp.sum(shrink * inner, axis=1, keepdims=True)
    weights = math.sqrt(members - 1) * shrink + mean_weight
    weights = weights + (1.0 - jnp.sum(weights, axis=0, keepdims=True)) / members
    weights_t = weights.T
    high = weights_t.astype(jnp.bfloat16)
    transform[0] = high
    transform[1] = (weights_t - high.astype(jnp.float32)).astype(jnp.bfloat16)

    for copy in late_copies:
        copy.wait()
    all_cells = jnp.concatenate(
        [cells[:, c, r].reshape(members, LANES) for c in range(3) for r in range(BAND)], axis=1
    )

    def analysed(peer):
        rows = pl.ds(pl.multiple_of(peer * group, group), group)
        total = jnp.dot(transform[0, rows, :], all_cells, preferred_element_type=jnp.float32)
        total += jnp.dot(transform[1, rows, :], all_cells, preferred_element_type=jnp.float32)
        return total.astype(jnp.bfloat16)

    def slabs(value):
        for c in range(3):
            for r in range(BAND):
                start = (c * BAND + r) * LANES
                yield c, r, value[:, start : start + LANES]

    back_copies = []
    for d in order:
        peer = lax.rem(me + d, n)
        for c, r, value in slabs(analysed(peer)):
            result[d, c, r] = value
        back_copies.append(
            send(result.at[d], out_ref.at[:, pl.ds(me * BAND, BAND)], back_send, back_recv, d, {"mem": peer})
        )
    for c, r, value in slabs(analysed(me)):
        out_ref[c, me * BAND + r] = value
    for copy in back_copies:
        copy.wait()


def on_device(
    sample_collection, layer_depth, obs_where, observed_values, obs_precision, loc_index, obs_count
):
    n = lax.axis_size("mem")
    group, _, _, rows, strip = sample_collection.shape
    slots = obs_where.shape[-1]
    x = sample_collection[:, :, 0].transpose(1, 2, 0, 3)
    vmem = pl.BlockSpec(memory_space=pltpu.VMEM)
    dma = pltpu.SemaphoreType.DMA
    bf16 = jnp.bfloat16
    halo = (2, 3, rows // (LANES // REACH), group, LANES)
    padded = (3, rows + 2 * MARGIN_WIDTH, group, LANES)
    block = (n, 3, BAND, group, LANES)
    out = pl.pallas_call(
        functools.partial(analysis_kernel, n),
        out_shape=jax.ShapeDtypeStruct((3, rows, group, LANES), bf16),
        in_specs=[vmem] * 7,
        out_specs=vmem,
        scratch_shapes=[
            pltpu.VMEM(halo, bf16),
            pltpu.VMEM(halo, bf16),
            pltpu.VMEM((2, rows, LANES), jnp.float32),
            pltpu.VMEM((n, 1, slots), jnp.int32),
            pltpu.VMEM((3, rows, group, LANES), bf16),
            pltpu.VMEM(padded, bf16),
            pltpu.VMEM(padded, bf16),
            pltpu.VMEM((n, group, LANES), bf16),
            pltpu.VMEM((n, group, LANES), bf16),
            pltpu.VMEM((n, group, slots), bf16),
            pltpu.VMEM((n, group, slots), bf16),
            pltpu.VMEM(block, bf16),
            pltpu.VMEM(block, bf16),
            pltpu.VMEM((2, n * group, n * group), bf16),
        ]
        + [dma((2,))] * 4
        + [dma((n,))] * 10,
        compiler_params=pltpu.CompilerParams(collective_id=0, has_side_effects=True),
    )(x, layer_depth[0], obs_where[0], observed_values[0], obs_precision[0], loc_index[0], obs_count)
    out = out.transpose(2, 0, 1, 3)
    return out.reshape(sample_collection.shape)


def solution(mesh):
    in_specs = (
        P("mem", None, None, None, "lon"),
        P(None, None, "lon"),
        P("mem", "lon", None),
        P("mem", "lon", None),
        P("mem", "lon", None),
        P("mem", "lon", None),
        P("mem", "lon"),
    )
    out_specs = P("mem", None, None, None, "lon")
    return jax.shard_map(
        on_device, mesh=mesh, in_specs=in_specs, out_specs=out_specs, check_vma=False
    )
```
